512 devices in a mesh: seq: 64 (over y, x, core), doc: 8 (over z).
Axes of the slice: x: 4, y: 8, z: 8, core: 2. Of those that a mesh axis runs over, the one named last changes fastest.
Arguments:
- grad_out: bfloat16 [8, 16384, 1024], P('doc', 'seq'), may hold values from -6 to 6
- pre_act: bfloat16 [8, 16384, 1024], P('doc', 'seq'), may hold values from -8 to 8
- word_of: int32 [8, 16384], P('doc', 'seq'), may hold values from 0 to 4095, as said below
- word_owner: int32 [8, 4096], P('doc'), may hold values from 0 to 63, as said below
- w_proj: bfloat16 [1024, 4096], P('seq', 'doc'), may hold values from -0.1875 to 0.1875
Outputs:
- word_grad: bfloat16 [8, 4096, 4096], P('doc', 'seq')
The draws below stay inside these ranges and needn't reach their ends.
Inputs may be any that keep to these rules, and one draw needn't show every extreme that they name: `word_of`: within a document the entries never fall, start at 0 and take every value up to 4095. The bytes of one device meet at most 127 different words, exactly that many on some device of every document; every device but the first begins inside the last word of the device before it. `word_owner`: the owner of word w depends only on w modulo 64, and different remainders have different owners, so every owner gets 64 words and at most 2 words met by one device share an owner.
All inputs are finite; a program needn't handle non-finite values.
Results may differ from the reference program's by a relative error of at most 0.0049.
Values may be sent and summed in bfloat16 or wider, within the bound.
No kernel may reach another device: no remote copies, remote signals or barrier semaphores. Data moves between devices by JAX's collectives and lax.ppermute only.
A program may use at most 64 MiB of HBM per device.

```python
import jax
import jax.numpy as jnp
from jax import lax

BYTE_DIM = 1024
MODEL_DIM = 4096
BYTES_DEV = 256
WCAP = 64
WORDS = 4096
SEQ_BYTES = 16384
DOCS = 8
N_SEQ = 64


def draw_word_of(key, part):
    spread = WCAP // N_SEQ

    def one_doc(doc_key):
        perm_key, shard_key = jax.random.split(jax.random.fold_in(doc_key, 11))
        offsets = 2 * jnp.arange(N_SEQ - 1, dtype=jnp.int32) - (N_SEQ - 2)
        shuffled = jax.random.permutation(perm_key, offsets)
        counts = jnp.concatenate([jnp.array([WCAP - 1], jnp.int32), WCAP + spread * shuffled])
        shard_keys = jax.random.split(shard_key, N_SEQ)

        def one_shard(one_key, count):
            order = jax.random.permutation(one_key, BYTES_DEV - 1)
            ranks = jnp.argsort(order).astype(jnp.int32)
            flags = (ranks < count).astype(jnp.int32)
            return jnp.concatenate([jnp.zeros((1,), jnp.int32), flags])
        starts = jax.vmap(one_shard)(shard_keys, counts)
        starts = starts.at[0, 0].set(1)
        return (jnp.cumsum(starts.reshape(-1)) - 1).astype(jnp.int32)
    return jax.vmap(one_doc)(jax.random.split(key, DOCS))


def draw_word_owner(key, part):

    def one_doc(doc_key):
        perm = jax.random.permutation(jax.random.fold_in(doc_key, 23), N_SEQ).astype(jnp.int32)
        return perm[jnp.arange(WORDS, dtype=jnp.int32) % N_SEQ]
    return jax.vmap(one_doc)(jax.random.split(key, DOCS))


def block_levels(rng, dims, shards, least, high):
    level = 1.0
    for axis_at, parts in shards:
        draws = jax.random.uniform(jax.random.fold_in(jax.random.fold_in(rng, 6), axis_at), (parts,), jnp.float32, least / len(shards), high / len(shards))
        level = level * jnp.repeat(jnp.exp(draws), dims[axis_at] // parts).reshape((-1,) + (1,) * (len(dims) - 1 - axis_at))
    return level


def normal_values(rng, extent, scale, limit, cuts=(), kind=jnp.bfloat16):
    result = scale * jax.random.normal(rng, extent, jnp.float32)
    if cuts:
        result = result * block_levels(rng, extent, cuts, -0.22, 0.18)
    return jnp.clip(result, -limit, limit).astype(kind)


def setup_inputs(seed: int = 0) -> dict:
    arg_keys = jax.random.split(jax.random.key(seed), 6)
    grad_out = normal_values(arg_keys[0], (DOCS, SEQ_BYTES, BYTE_DIM), 1.0, 6.0, ((0, 8), (1, 64)))
    pre_act = normal_values(arg_keys[1], (DOCS, SEQ_BYTES, BYTE_DIM), 1.5, 8.0, ((0, 8), (1, 64)))
    word_of = draw_word_of(jax.random.fold_in(arg_keys[5], 71), 0)
    word_owner = draw_word_owner(jax.random.fold_in(arg_keys[5], 71), 0)
    w_proj = normal_values(arg_keys[4], (BYTE_DIM, MODEL_DIM), BYTE_DIM ** -0.5, 0.1875, ((0, 64), (1, 8)))
    return {"grad_out": grad_out, "pre_act": pre_act, "word_of": word_of, "word_owner": word_owner, "w_proj": w_proj}


inv_root_two = 0.7071067811865476
inv_root_tau = 0.3989422804014327


def slope_of(pre):
    value = pre.astype(jnp.float32)
    return 0.5 * (1.0 + jax.scipy.special.erf(value * inv_root_two)) + value * jnp.exp(-0.5 * value * value) * inv_root_tau


def reference(grad_out, pre_act, word_of, word_owner, w_proj):
    weight = w_proj.astype(jnp.float32)

    def one_doc(items):
        cotangent, pre, word_ids, owners = items
        g_pre = (cotangent.astype(jnp.float32) * slope_of(pre)).astype(jnp.bfloat16).astype(jnp.float32)
        sums = jax.ops.segment_sum(g_pre, word_ids, num_segments=WORDS)
        word_sum = jnp.dot(sums, weight, precision=lax.Precision.HIGHEST)
        target = owners * WCAP + jnp.arange(WORDS, dtype=jnp.int32) // N_SEQ
        packed = jnp.zeros((WORDS, MODEL_DIM), jnp.float32).at[target.astype(jnp.int32)].set(word_sum)
        return packed.astype(jnp.bfloat16)

    return lax.map(one_doc, (grad_out, pre_act, word_of, word_owner))
```

```python
import jax
import jax.numpy as jnp
from jax import lax
from jax.experimental import pallas as pl
from jax.experimental.pallas import tpu as pltpu
from jax.sharding import PartitionSpec as P

inv_root_two = 0.7071067811865476
inv_root_tau = 0.3989422804014327
BF16 = jnp.bfloat16
F32 = jnp.float32
LANES = 128


def slope_of(value):
    return (
        0.5 * (1.0 + lax.erf(value * inv_root_two))
        + value * jnp.exp(-0.5 * value * value) * inv_root_tau
    )


def word_sums_kernel(n_seq, word_ref, owner_ref, grad_ref, pre_ref, w_ref, out_ref):
    slots = 2 * n_seq
    width = grad_ref.shape[1]
    words = word_ref[...]
    rank = words // n_seq
    row = lax.broadcasted_iota(jnp.int32, (slots, LANES), 0)
    lane = lax.broadcasted_iota(jnp.int32, (slots, LANES), 1)
    owned = (owner_ref[...] == row // 2) & (lane < n_seq)
    remainder = jnp.sum(jnp.where(owned, lane, 0).astype(F32), axis=1, keepdims=True)
    parity = lax.broadcasted_iota(jnp.int32, (slots, 1), 0) % 2
    match = (words % n_seq == remainder.astype(jnp.int32)) & (rank % 2 == parity)
    ids = jnp.max(jnp.where(match, rank, 0).astype(F32), axis=1, keepdims=True)
    picks = jnp.where(match, 1.0, 0.0).astype(BF16)
    step = 256
    for at in range(0, width, step):
        cols = slice(at, at + step)
        g_pre = (grad_ref[:, cols].astype(F32) * slope_of(pre_ref[:, cols].astype(F32))).astype(BF16)
        out_ref[:, cols] = jnp.dot(picks, g_pre, preferred_element_type=F32).astype(BF16)
    out_ref[:, width : width + LANES] = jnp.broadcast_to(ids, (slots, LANES)).astype(BF16)
    depth = w_ref.shape[0]
    for at in range(0, slots, depth):
        out_ref[at : at + depth, width + LANES :] = w_ref[...]


def own_rows_kernel(per_owner, width, got_ref, out_ref):
    slots = got_ref.shape[0]
    ids = jnp.transpose(got_ref[:, width : width + LANES].astype(F32))[0:1, :]
    rows = lax.broadcasted_iota(jnp.int32, (per_owner, slots), 0)
    picks = jnp.where(rows == ids.astype(jnp.int32), 1.0, 0.0).astype(BF16)
    source = lax.broadcasted_iota(jnp.int32, (LANES, LANES), 0)
    target = lax.broadcasted_iota(jnp.int32, (LANES, LANES), 1)
    moved = (source // 2 % 8) * 16 + (source // 16) * 2 + source % 2
    order = jnp.where(moved == target, 1.0, 0.0).astype(BF16)
    for at in range(0, width, LANES):
        cols = slice(at, at + LANES)
        summed = jnp.dot(picks, got_ref[:, cols], preferred_element_type=F32).astype(BF16)
        summed = jnp.dot(summed, order, preferred_element_type=F32).astype(BF16)
        for copy in range(out_ref.shape[0]):
            out_ref[copy, :, cols] = summed


def project_kernel(masks, rows_ref, *refs):
    pieces, out_ref, w_ref = refs[:-2], refs[-2], refs[-1]
    inner = len(masks)
    depth = LANES // inner
    outer = w_ref.shape[0] // LANES
    here = lax.axis_index("seq") % inner
    each = inner // len(pieces)
    for slot, mask in enumerate(masks):
        source = pieces[slot // each]
        place = (here ^ mask) * depth
        for tile in range(outer):
            start = pl.multiple_of(tile * LANES + place, depth)
            at = (slot % each) * LANES + tile * depth
            w_ref[pl.ds(start, depth), :] = source[at : at + depth, :]
    out_ref[...] = jnp.dot(rows_ref[...], w_ref[...], preferred_element_type=F32).astype(BF16)


def lay_out_kernel(back_ref, out_ref):
    cols = back_ref.shape[2]
    for block in range(back_ref.shape[0]):
        out_ref[:, block * cols : (block + 1) * cols] = back_ref[block]


def shards(grad_out, pre_act, word_of, word_owner, w_proj):
    n_seq = lax.axis_size("seq")
    n_doc = lax.axis_size("doc")
    width = grad_out.shape[2]
    slots = 2 * n_seq
    per_owner = word_owner.shape[1] // n_seq
    depth, cols = w_proj.shape
    total = width + LANES + cols
    params = pltpu.CompilerParams(vmem_limit_bytes=VMEM_LIMIT)

    sums = pl.pallas_call(
        lambda *refs: word_sums_kernel(n_seq, *refs),
        out_shape=jax.ShapeDtypeStruct((slots, total), BF16),
        grid=(1,),
        in_specs=[
            pl.BlockSpec(word_of.shape, lambda i: (0, 0)),
            pl.BlockSpec((1, LANES), lambda i: (0, 0)),
            pl.BlockSpec(grad_out.shape[1:], lambda i: (0, 0)),
            pl.BlockSpec(pre_act.shape[1:], lambda i: (0, 0)),
            pl.BlockSpec(w_proj.shape, lambda i: (0, 0)),
        ],
        out_specs=pl.BlockSpec((slots, total), lambda i: (0, 0)),
        compiler_params=params,
        cost_estimate=pl.CostEstimate(flops=20_000_000, bytes_accessed=3_000_000, transcendentals=500_000),
        name="word_sums",
    )(word_of, word_owner, grad_out[0], pre_act[0], w_proj)
    got = lax.all_to_all(
        sums.reshape(n_seq, 2, total), "seq", 0, 0, tiled=True
    ).reshape(slots, total)

    rows = pl.pallas_call(
        lambda *refs: own_rows_kernel(per_owner, width, *refs),
        out_shape=jax.ShapeDtypeStruct((n_doc, per_owner, width), BF16),
        compiler_params=params,
        cost_estimate=pl.CostEstimate(flops=20_000_000, bytes_accessed=1_500_000, transcendentals=0),
        name="own_rows",
    )(got)
    rows = lax.all_to_all(rows, "doc", 0, 0, tiled=True).reshape(n_doc * per_owner, width)

    have = got[:, width + LANES :]
    masks = [0]
    for bit in BITS[:-1]:
        other = lax.ppermute(have, "seq", [(i, i ^ bit) for i in range(n_seq)])
        have = jnp.concatenate([have, other], axis=0)
        masks += [mask ^ bit for mask in masks]
    other = lax.ppermute(have, "seq", [(i, i ^ BITS[-1]) for i in range(n_seq)])
    masks += [mask ^ BITS[-1] for mask in masks]

    part = pl.pallas_call(
        lambda *refs: project_kernel(masks, *refs),
        out_shape=jax.ShapeDtypeStruct((n_doc * per_owner, cols), BF16),
        scratch_shapes=[pltpu.VMEM((width, cols), BF16)],
        compiler_params=params,
        cost_estimate=pl.CostEstimate(flops=600_000_000, bytes_accessed=2_500_000, transcendentals=0),
        name="project",
    )(rows, have, other)
    back = lax.all_to_all(part.reshape(n_doc, per_owner, cols), "doc", 0, 0, tiled=True)
    out = pl.pallas_call(
        lay_out_kernel,
        out_shape=jax.ShapeDtypeStruct((per_owner, n_doc * cols), BF16),
        compiler_params=params,
        name="lay_out",
    )(back)
    return out[None]


BITS = (4, 2, 1)
VMEM_LIMIT = 16 * 1024 * 1024


def solution(mesh):
    return jax.shard_map(
        shards,
        mesh=mesh,
        in_specs=(
            P("doc", "seq", None),
            P("doc", "seq", None),
            P("doc", "seq"),
            P("doc", None),
            P("seq", "doc"),
        ),
        out_specs=P("doc", "seq", None),
        check_vma=False,
    )
```

```python
import jax
import jax.numpy as jnp
from jax import lax
from jax.experimental import pallas as pl
from jax.experimental.pallas import tpu as pltpu
from jax.sharding import PartitionSpec as P

inv_root_two = 0.7071067811865476
inv_root_tau = 0.3989422804014327
BF16 = jnp.bfloat16
F32 = jnp.float32
LANES = 128


def slope_of(value):
    return (
        0.5 * (1.0 + lax.erf(value * inv_root_two))
        + value * jnp.exp(-0.5 * value * value) * inv_root_tau
    )


def word_sums_kernel(n_seq, word_ref, owner_ref, grad_ref, pre_ref, out_ref):
    slots = 2 * n_seq
    width = grad_ref.shape[1]
    words = word_ref[...]
    rank = words // n_seq
    row = lax.broadcasted_iota(jnp.int32, (slots, LANES), 0)
    lane = lax.broadcasted_iota(jnp.int32, (slots, LANES), 1)
    owned = (owner_ref[...] == row // 2) & (lane < n_seq)
    remainder = jnp.sum(jnp.where(owned, lane, 0).astype(F32), axis=1, keepdims=True)
    parity = lax.broadcasted_iota(jnp.int32, (slots, 1), 0) % 2
    match = (words % n_seq == remainder.astype(jnp.int32)) & (rank % 2 == parity)
    ids = jnp.max(jnp.where(match, rank, 0).astype(F32), axis=1, keepdims=True)
    picks = jnp.where(match, 1.0, 0.0).astype(BF16)
    step = 256
    for at in range(0, width, step):
        cols = slice(at, at + step)
        g_pre = (grad_ref[:, cols].astype(F32) * slope_of(pre_ref[:, cols].astype(F32))).astype(BF16)
        out_ref[:, cols] = jnp.dot(picks, g_pre, preferred_element_type=F32).astype(BF16)
    out_ref[:, width : width + LANES] = jnp.broadcast_to(ids, (slots, LANES)).astype(BF16)


def pack_kernel(sums_ref, w_ref, out_ref):
    slots, width = sums_ref.shape
    blocks, depth, cols = w_ref.shape
    out_ref[:, :width] = sums_ref[...]
    out_row = lax.broadcasted_iota(jnp.int32, (slots, blocks * depth), 0)
    w_row = lax.broadcasted_iota(jnp.int32, (slots, blocks * depth), 1)
    block = out_row // 16 % 2 * 4 + out_row // 4 % 4
    inner = out_row // 2 % 2 * 4 + out_row % 2
    flat = w_ref[...].astype(F32).reshape(blocks * depth, cols).astype(BF16)
    for h in range(2):
        chosen = jnp.where(w_row == block * depth + inner + 2 * h, 1.0, 0.0).astype(BF16)
        first = width + h * cols
        out_ref[:, first : first + cols] = jnp.dot(
            chosen, flat, preferred_element_type=F32
        ).astype(BF16)


def own_rows_kernel(per_owner, width, got_ref, out_ref):
    slots = got_ref.shape[0]
    ids = jnp.transpose(got_ref[:, width : width + LANES].astype(F32))[0:1, :]
    rows = lax.broadcasted_iota(jnp.int32, (per_owner, slots), 0)
    picks = jnp.where(rows == ids.astype(jnp.int32), 1.0, 0.0).astype(BF16)
    source = lax.broadcasted_iota(jnp.int32, (LANES, LANES), 0)
    target = lax.broadcasted_iota(jnp.int32, (LANES, LANES), 1)
    moved = (source // 2 % 8) * 16 + (source // 16) * 2 + source % 2
    order = jnp.where(moved == target, 1.0, 0.0).astype(BF16)
    for at in range(0, width, LANES):
        cols = slice(at, at + LANES)
        summed = jnp.dot(picks, got_ref[:, cols], preferred_element_type=F32).astype(BF16)
        summed = jnp.dot(summed, order, preferred_element_type=F32).astype(BF16)
        for copy in range(out_ref.shape[0]):
            out_ref[copy, :, cols] = summed


def project_kernel(masks, rows_ref, *refs):
    pieces, out_ref, w_ref = refs[:-2], refs[-2], refs[-1]
    cols = w_ref.shape[1]
    me = lax.axis_index("seq")
    here = lax.axis_index("doc") % 2 * 2 + me % 2
    each = len(masks) // len(pieces)
    depth = LANES // (2 * len(masks))
    for slot, mask in enumerate(masks):
        source = pieces[slot // each]
        place = (here ^ mask) * (2 * depth)
        for h in range(2):
            for tile in range(w_ref.shape[0] // LANES):
                start = pl.multiple_of(tile * LANES + h * depth + place, depth)
                at = (slot % each) * LANES + tile * depth
                w_ref[pl.ds(start, depth), :] = source[at : at + depth, h * cols : (h + 1) * cols]
    out_ref[...] = jnp.dot(rows_ref[...], w_ref[...], preferred_element_type=F32).astype(BF16)


def lay_out_kernel(back_ref, out_ref):
    cols = back_ref.shape[2]
    for block in range(back_ref.shape[0]):
        out_ref[:, block * cols : (block + 1) * cols] = back_ref[block]


def shards(grad_out, pre_act, word_of, word_owner, w_proj):
    n_seq = lax.axis_size("seq")
    n_doc = lax.axis_size("doc")
    width = grad_out.shape[2]
    slots = 2 * n_seq
    per_owner = word_owner.shape[1] // n_seq
    depth, cols = w_proj.shape
    total = width + LANES + 2 * cols
    groups = [
        [32 * y2 + 16 * y1 + 8 * y0 + 2 * x + c for y0 in range(2) for x in range(4)]
        for y2 in range(2)
        for y1 in range(2)
        for c in range(2)
    ]
    w_docs = lax.all_to_all(
        jnp.broadcast_to(
            w_proj.reshape(1, 2, depth // 2, cols), (n_doc // 2, 2, depth // 2, cols)
        ).reshape(n_doc, depth // 2, cols),
        "doc", 0, 0, tiled=True,
    )
    params = pltpu.CompilerParams(vmem_limit_bytes=VMEM_LIMIT)

    sums = pl.pallas_call(
        lambda *refs: word_sums_kernel(n_seq, *refs),
        out_shape=jax.ShapeDtypeStruct((slots, width + LANES), BF16),
        grid=(1,),
        in_specs=[
            pl.BlockSpec(word_of.shape, lambda i: (0, 0)),
            pl.BlockSpec((1, LANES), lambda i: (0, 0)),
            pl.BlockSpec(grad_out.shape[1:], lambda i: (0, 0)),
            pl.BlockSpec(pre_act.shape[1:], lambda i: (0, 0)),
        ],
        out_specs=pl.BlockSpec((slots, width + LANES), lambda i: (0, 0)),
        compiler_params=params,
        cost_estimate=pl.CostEstimate(flops=20_000_000, bytes_accessed=3_000_000, transcendentals=500_000),
        name="word_sums",
    )(word_of, word_owner, grad_out[0], pre_act[0])
    packed = pl.pallas_call(
        pack_kernel,
        out_shape=jax.ShapeDtypeStruct((slots, total), BF16),
        compiler_params=params,
        cost_estimate=pl.CostEstimate(flops=20_000_000, bytes_accessed=1_000_000, transcendentals=0),
        name="pack",
    )(sums, w_docs)
    got = lax.all_to_all(
        packed.reshape(n_seq, 2, total), "seq", 0, 0, tiled=True
    ).reshape(slots, total)

    rows = pl.pallas_call(
        lambda *refs: own_rows_kernel(per_owner, width, *refs),
        out_shape=jax.ShapeDtypeStruct((n_doc, per_owner, width), BF16),
        compiler_params=params,
        cost_estimate=pl.CostEstimate(flops=20_000_000, bytes_accessed=1_500_000, transcendentals=0),
        name="own_rows",
    )(got)
    rows = lax.all_to_all(rows, "seq", 0, 0, tiled=True, axis_index_groups=groups).reshape(n_doc * per_owner, width)

    have = got[:, width + LANES :]
    other = lax.ppermute(have, "doc", [(i, i ^ 1) for i in range(n_doc)])
    have = jnp.concatenate([have, other], axis=0)
    other = lax.ppermute(have, "seq", [(i, i ^ 1) for i in range(n_seq)])
    masks = [0, 2, 1, 3]

    part = pl.pallas_call(
        lambda *refs: project_kernel(masks, *refs),
        out_shape=jax.ShapeDtypeStruct((n_doc * per_owner, cols), BF16),
        scratch_shapes=[pltpu.VMEM((width, cols), BF16)],
        compiler_params=params,
        cost_estimate=pl.CostEstimate(flops=600_000_000, bytes_accessed=2_500_000, transcendentals=0),
        name="project",
    )(rows, have, other)
    back = lax.all_to_all(part.reshape(n_doc, per_owner, cols), "seq", 0, 0, tiled=True, axis_index_groups=groups)
    out = pl.pallas_call(
        lay_out_kernel,
        out_shape=jax.ShapeDtypeStruct((per_owner, n_doc * cols), BF16),
        compiler_params=params,
        name="lay_out",
    )(back)
    return out[None]


VMEM_LIMIT = 16 * 1024 * 1024


def solution(mesh):
    return jax.shard_map(
        shards,
        mesh=mesh,
        in_specs=(
            P("doc", "seq", None),
            P("doc", "seq", None),
            P("doc", "seq"),
            P("doc", None),
            P("seq", "doc"),
        ),
        out_specs=P("doc", "seq", None),
        check_vma=False,
    )
```

```python
import jax
import jax.numpy as jnp
from jax import lax
from jax.experimental import pallas as pl
from jax.experimental.pallas import tpu as pltpu
from jax.sharding import PartitionSpec as P


inv_root_two = 0.7071067811865476
inv_root_tau = 0.3989422804014327
BF16 = jnp.bfloat16
F32 = jnp.float32
LANES = 128


def slope_of(value):
    return (
        0.5 * (1.0 + lax.erf(value * inv_root_two))
        + value * jnp.exp(-0.5 * value * value) * inv_root_tau
    )


def word_sums_kernel(n_seq, word_hbm, owner_hbm, grad_hbm, pre_hbm, keep_ref, send_ref, *scratch):
    word_ref, owner_ref, grad_ref, pre_ref, small_sem, grad_sem, pre_sem = scratch
    half = n_seq
    width = grad_ref.shape[1]
    step = 2 * LANES
    chunks = width // step
    small = [
        pltpu.make_async_copy(word_hbm, word_ref, small_sem.at[0]),
        pltpu.make_async_copy(owner_hbm.at[:, :LANES], owner_ref, small_sem.at[1]),
    ]
    large = []
    for copy in small:
        copy.start()
    for chunk in range(chunks):
        cols = pl.ds(chunk * step, step)
        large.append(
            (
                pltpu.make_async_copy(pre_hbm.at[:, cols], pre_ref.at[:, cols], pre_sem.at[chunk]),
                pltpu.make_async_copy(grad_hbm.at[:, cols], grad_ref.at[:, cols], grad_sem.at[chunk]),
            )
        )
        for copy in large[-1]:
            copy.start()
    source = lax.broadcasted_iota(jnp.int32, (step, step), 0)
    target = lax.broadcasted_iota(jnp.int32, (step, step), 1)
    moved = (
        source // 16 % 2 * 128
        + source // 8 % 2 * 64
        + source // 2 % 4 * 16
        + source // 32 * 2
        + source % 2
    )
    order = jnp.where(moved == target, 1.0, 0.0).astype(BF16)
    core = lax.axis_index("seq") % 2
    row = lax.broadcasted_iota(jnp.int32, (2 * half, LANES), 0)
    lane = lax.broadcasted_iota(jnp.int32, (2 * half, LANES), 1)
    owner = row % half // 2 * 2 + (core ^ row // half)
    for copy in small:
        copy.wait()
    words = word_ref[...]
    rank = words // n_seq
    owned = (owner_ref[...] == owner) & (lane < n_seq)
    remainder = jnp.sum(jnp.where(owned, lane, 0).astype(F32), axis=1, keepdims=True)
    parity = lax.broadcasted_iota(jnp.int32, (2 * half, 1), 0) % 2
    match = (words % n_seq == remainder.astype(jnp.int32)) & (rank % 2 == parity)
    ids = jnp.max(jnp.where(match, rank, 0).astype(F32), axis=1, keepdims=True)
    picks = jnp.where(match, 1.0, 0.0).astype(BF16)
    wide = jnp.broadcast_to(ids, (2 * half, LANES)).astype(BF16)
    keep_ref[:, width:] = wide[:half]
    send_ref[:, width:] = wide[half:]
    for chunk in range(chunks):
        cols = slice(chunk * step, (chunk + 1) * step)
        for copy in large[chunk]:
            copy.wait()
        g_pre = (grad_ref[:, cols].astype(F32) * slope_of(pre_ref[:, cols].astype(F32))).astype(BF16)
        summed = jnp.dot(picks, g_pre, preferred_element_type=F32).astype(BF16)
        summed = jnp.dot(summed, order, preferred_element_type=F32).astype(BF16)
        keep_ref[:, cols] = summed[:half]
        send_ref[:, cols] = summed[half:]


def pack_kernel(keep_ref, other_ref, w_ref, out_ref):
    rows, width = keep_ref.shape
    blocks, depth, cols = w_ref.shape
    out_ref[:, :width] = keep_ref[...]
    out_ref[:, width : 2 * width] = other_ref[...]
    out_row = lax.broadcasted_iota(jnp.int32, (rows, blocks * depth), 0)
    w_row = lax.broadcasted_iota(jnp.int32, (rows, blocks * depth), 1)
    first = (out_row // 8 % 2 * 4 + out_row // 2 % 4) * depth + out_row % 2
    flat = w_ref[...].astype(F32).reshape(blocks * depth, cols).astype(BF16)
    for h in range(depth // 2):
        chosen = jnp.where(w_row == first + 2 * h, 1.0, 0.0).astype(BF16)
        at = 2 * width + h * cols
        out_ref[:, at : at + cols] = jnp.dot(
            chosen, flat, preferred_element_type=F32
        ).astype(BF16)


def own_rows_kernel(per_owner, width, got_ref, out_ref):
    slots = got_ref.shape[0]
    diagonal = lax.broadcasted_iota(jnp.int32, (slots, LANES), 0) == lax.broadcasted_iota(
        jnp.int32, (slots, LANES), 1
    )
    rows = lax.broadcasted_iota(jnp.int32, (per_owner, slots), 0)
    summed = None
    for at in (0, width + LANES):
        wide = got_ref[:, at + width : at + width + LANES].astype(F32)
        ids = jnp.sum(jnp.where(diagonal, wide, 0.0), axis=0, keepdims=True)[:, :slots]
        picks = jnp.where(rows == ids.astype(jnp.int32), 1.0, 0.0).astype(BF16)
        part = jnp.dot(picks, got_ref[:, at : at + width], preferred_element_type=F32)
        summed = part if summed is None else summed + part
    summed = summed.astype(BF16)
    for copy in range(out_ref.shape[0]):
        out_ref[copy] = summed


def project_kernel(rows_ref, mine_ref, theirs_ref, out_ref, w_ref):
    cols = w_ref.shape[1]
    parts = mine_ref.shape[1] // cols
    half = mine_ref.shape[0] // 2
    core = lax.axis_index("seq") % 2
    plane = lax.axis_index("doc") % 2
    for c, source in enumerate((mine_ref, theirs_ref)):
        for z in range(2):
            place = (core ^ c) * 128 + (plane ^ z) * 64
            for tile in range(half // 16):
                at = z * half + tile * 16
                for h in range(parts):
                    start = pl.multiple_of(tile * 256 + h * 16 + place, 16)
                    w_ref[pl.ds(start, 16), :] = source[at : at + 16, h * cols : (h + 1) * cols]
    out_ref[...] = jnp.dot(rows_ref[...], w_ref[...], preferred_element_type=F32).astype(BF16)


def lay_out_kernel(back_ref, out_ref):
    cols = back_ref.shape[2]
    for block in range(back_ref.shape[0]):
        out_ref[:, block * cols : (block + 1) * cols] = back_ref[block]


def step(grad_out, pre_act, word_of, word_owner, w_proj):
    n_seq = lax.axis_size("seq")
    n_doc = lax.axis_size("doc")
    n_chip = n_seq // 2
    bytes_here, width = grad_out.shape[1:]
    per_owner = word_owner.shape[1] // n_seq
    depth, cols = w_proj.shape
    part = width + LANES
    total = 2 * part + depth // 4 * cols
    groups = [
        [32 * y2 + 16 * y1 + 8 * y0 + 2 * x + c for y0 in range(2) for x in range(4)]
        for y2 in range(2)
        for y1 in range(2)
        for c in range(2)
    ]
    same_core = [[2 * chip + c for chip in range(n_chip)] for c in range(2)]
    across = [(i, i ^ 1) for i in range(n_seq)]
    params = pltpu.CompilerParams(vmem_limit_bytes=VMEM_LIMIT)

    w_docs = lax.all_to_all(
        jnp.broadcast_to(
            w_proj.reshape(1, 2, depth // 2, cols), (n_doc // 2, 2, depth // 2, cols)
        ).reshape(n_doc, depth // 2, cols),
        "doc", 0, 0, tiled=True,
    )
    chunks = width // (2 * LANES)
    inputs = [
        pltpu.with_memory_space_constraint(x, pltpu.HBM)
        for x in (word_of, word_owner, grad_out[0], pre_act[0])
    ]
    keep, send = pl.pallas_call(
        lambda *refs: word_sums_kernel(n_seq, *refs),
        out_shape=[jax.ShapeDtypeStruct((n_seq, part), BF16)] * 2,
        in_specs=[pl.BlockSpec(memory_space=pltpu.HBM)] * 4,
        scratch_shapes=[
            pltpu.VMEM((1, bytes_here), jnp.int32),
            pltpu.VMEM((1, LANES), jnp.int32),
            pltpu.VMEM((bytes_here, width), BF16),
            pltpu.VMEM((bytes_here, width), BF16),
            pltpu.SemaphoreType.DMA((2,)),
            pltpu.SemaphoreType.DMA((chunks,)),
            pltpu.SemaphoreType.DMA((chunks,)),
        ],
        compiler_params=params,
        cost_estimate=pl.CostEstimate(flops=20_000_000, bytes_accessed=3_000_000, transcendentals=500_000),
        name="word_sums",
    )(*inputs)
    other = lax.ppermute(send, "seq", across)
    packed = pl.pallas_call(
        pack_kernel,
        out_shape=jax.ShapeDtypeStruct((n_seq, total), BF16),
        compiler_params=params,
        cost_estimate=pl.CostEstimate(flops=20_000_000, bytes_accessed=1_000_000, transcendentals=0),
        name="pack",
    )(keep, other, w_docs)
    got = lax.all_to_all(
        packed.reshape(n_chip, 2, total), "seq", 0, 0, tiled=True, axis_index_groups=same_core
    ).reshape(n_seq, total)

    rows = pl.pallas_call(
        lambda *refs: own_rows_kernel(per_owner, width, *refs),
        out_shape=jax.ShapeDtypeStruct((n_doc, per_owner, width), BF16),
        compiler_params=params,
        cost_estimate=pl.CostEstimate(flops=20_000_000, bytes_accessed=1_500_000, transcendentals=0),
        name="own_rows",
    )(got)
    rows = lax.all_to_all(rows, "seq", 0, 0, tiled=True, axis_index_groups=groups)

    mine = got[:, 2 * part :]
    theirs = lax.ppermute(mine, "doc", [(i, i ^ 1) for i in range(n_doc)])
    mine = jnp.concatenate([mine, theirs], axis=0)
    theirs = lax.ppermute(mine, "seq", across)

    out = pl.pallas_call(
        project_kernel,
        out_shape=jax.ShapeDtypeStruct((n_doc * per_owner, cols), BF16),
        scratch_shapes=[pltpu.VMEM((width, cols), BF16)],
        compiler_params=params,
        cost_estimate=pl.CostEstimate(flops=600_000_000, bytes_accessed=2_500_000, transcendentals=0),
        name="project",
    )(rows.reshape(n_doc * per_owner, width), mine, theirs)
    back = lax.all_to_all(
        out.reshape(n_doc, per_owner, cols), "seq", 0, 0, tiled=True, axis_index_groups=groups
    )
    out = pl.pallas_call(
        lay_out_kernel,
        out_shape=jax.ShapeDtypeStruct((per_owner, n_doc * cols), BF16),
        compiler_params=params,
        name="lay_out",
    )(back)
    return out[None]


VMEM_LIMIT = 16 * 1024 * 1024


def solution(mesh):
    return jax.shard_map(
        step,
        mesh=mesh,
        in_specs=(
            P("doc", "seq", None),
            P("doc", "seq", None),
            P("doc", "seq"),
            P("doc", None),
            P("seq", "doc"),
        ),
        out_specs=P("doc", "seq", None),
        check_vma=False,
    )
```

```python
import jax
import jax.numpy as jnp
from jax import lax
from jax.experimental import pallas as pl
from jax.experimental.pallas import tpu as pltpu
from jax.sharding import PartitionSpec as P


inv_root_two = 0.7071067811865476
inv_root_tau = 0.3989422804014327
BF16 = jnp.bfloat16
F32 = jnp.float32
LANES = 128


def slope_of(value):
    return (
        0.5 * (1.0 + lax.erf(value * inv_root_two))
        + value * jnp.exp(-0.5 * value * value) * inv_root_tau
    )


def load_kernel(word_hbm, owner_hbm, grad_hbm, pre_hbm, w_hbm, word_ref, owner_ref, grad_ref, pre_ref, sent_hbm, w_ref, sems):
    half = w_ref.shape[0] // 2
    first = [pltpu.make_async_copy(w_hbm, w_ref, sems.at[0])]
    loads = [
        pltpu.make_async_copy(word_hbm, word_ref, sems.at[1]),
        pltpu.make_async_copy(owner_hbm.at[:, :LANES], owner_ref, sems.at[2]),
        pltpu.make_async_copy(pre_hbm, pre_ref, sems.at[3]),
        pltpu.make_async_copy(grad_hbm, grad_ref, sems.at[4]),
    ]
    for copy in first:
        copy.start()
    for copy in loads:
        copy.start()
    for copy in first:
        copy.wait()
    stores = [
        pltpu.make_async_copy(w_ref.at[pl.ds(d % 2 * half, half), :], sent_hbm.at[i], sems.at[5 + i])
        for i, d in enumerate(DOC_ORDER)
    ]
    for copy in stores:
        copy.start()
    for copy in loads + stores:
        copy.wait()


def word_sums_kernel(n_seq, word_ref, owner_ref, grad_ref, pre_ref, keep_ref, send_ref):
    half = n_seq
    width = grad_ref.shape[1]
    step = 2 * LANES
    chunks = width // step
    source = lax.broadcasted_iota(jnp.int32, (step, step), 0)
    target = lax.broadcasted_iota(jnp.int32, (step, step), 1)
    moved = (
        source // 16 % 2 * 128
        + source // 8 % 2 * 64
        + source // 2 % 4 * 16
        + (7 - source // 32 if REVERSE_SEQ else source // 32) * 2
        + source % 2
    )
    order = jnp.where(moved == target, 1.0, 0.0).astype(BF16)
    core = lax.axis_index("seq") % 2
    row = lax.broadcasted_iota(jnp.int32, (2 * half, LANES), 0)
    lane = lax.broadcasted_iota(jnp.int32, (2 * half, LANES), 1)
    chip = row % half // 2
    chip = half // 2 - 1 - chip if REVERSE_SEQ else chip
    owner = chip * 2 + (core ^ row // half)
    words = word_ref[...]
    rank = words // n_seq
    owned = (owner_ref[...] == owner) & (lane < n_seq)
    remainder = jnp.sum(jnp.where(owned, lane, 0).astype(F32), axis=1, keepdims=True)
    parity = lax.broadcasted_iota(jnp.int32, (2 * half, 1), 0) % 2
    match = (words % n_seq == remainder.astype(jnp.int32)) & (rank % 2 == parity)
    ids = jnp.max(jnp.where(match, rank, 0).astype(F32), axis=1, keepdims=True)
    picks = jnp.where(match, 1.0, 0.0).astype(BF16)
    wide = jnp.broadcast_to(ids, (2 * half, LANES)).astype(BF16)
    keep_ref[:, width:] = wide[:half]
    send_ref[:, width:] = wide[half:]
    for chunk in range(chunks):
        cols = slice(chunk * step, (chunk + 1) * step)
        g_pre = (grad_ref[:, cols].astype(F32) * slope_of(pre_ref[:, cols].astype(F32))).astype(BF16)
        summed = jnp.dot(picks, g_pre, preferred_element_type=F32).astype(BF16)
        summed = jnp.dot(summed, order, preferred_element_type=F32).astype(BF16)
        keep_ref[:, cols] = summed[:half]
        send_ref[:, cols] = summed[half:]


def pack_kernel(keep_ref, other_ref, w_ref, out_ref):
    rows = keep_ref.shape[0]
    width = keep_ref.shape[1] - LANES
    blocks, depth, cols = w_ref.shape
    out_ref[:, :width] = keep_ref[:, :width]
    out_ref[:, width : 2 * width] = other_ref[:, :width]
    lane = lax.broadcasted_iota(jnp.int32, (rows, LANES), 1)
    ids = [ref[:, width:].astype(F32) for ref in (keep_ref, other_ref)]
    out_ref[:, 2 * width : 2 * width + LANES] = jnp.where(lane < rows, *ids).astype(BF16)
    out_row = lax.broadcasted_iota(jnp.int32, (rows, blocks * depth), 0)
    w_row = lax.broadcasted_iota(jnp.int32, (rows, blocks * depth), 1)
    chip = out_row // 2
    chip = rows // 2 - 1 - chip if REVERSE_SEQ else chip
    block = chip // 4 % 2 * 4 + chip % 4
    place = sum(jnp.where(block == d, i, 0) for i, d in enumerate(DOC_ORDER))
    first = place * depth + out_row % 2
    flat = w_ref[...].astype(F32).reshape(blocks * depth, cols).astype(BF16)
    for h in range(depth // 2):
        chosen = jnp.where(w_row == first + 2 * h, 1.0, 0.0).astype(BF16)
        at = 2 * width + LANES + h * cols
        out_ref[:, at : at + cols] = jnp.dot(
            chosen, flat, preferred_element_type=F32
        ).astype(BF16)


def own_rows_kernel(per_owner, width, got_ref, out_ref):
    slots = got_ref.shape[0]
    slot = lax.broadcasted_iota(jnp.int32, (slots, LANES), 0)
    lane = lax.broadcasted_iota(jnp.int32, (slots, LANES), 1)
    wide = got_ref[:, 2 * width : 2 * width + LANES].astype(F32)
    ids = jnp.sum(jnp.where(slot == lane % slots, wide, 0.0), axis=0, keepdims=True)
    rows = lax.broadcasted_iota(jnp.int32, (per_owner, LANES), 0)
    picks = jnp.where(rows == ids.astype(jnp.int32), 1.0, 0.0).astype(BF16)
    summed = jnp.dot(
        picks[:, :slots], got_ref[:, :width], preferred_element_type=F32
    ) + jnp.dot(picks[:, slots:], got_ref[:, width : 2 * width], preferred_element_type=F32)
    summed = summed.astype(BF16)
    for copy in range(out_ref.shape[0]):
        out_ref[copy] = summed


def project_kernel(rows_ref, mine_ref, theirs_ref, out_ref, w_ref):
    cols = w_ref.shape[1]
    parts = mine_ref.shape[1] // cols
    half = mine_ref.shape[0] // 2
    core = lax.axis_index("seq") % 2
    plane = lax.axis_index("doc") % 2
    for c, source in enumerate((mine_ref, theirs_ref)):
        for z in range(2):
            place = (core ^ c) * 128 + (plane ^ z) * 64
            for tile in range(half // 16):
                at = z * half + tile * 16
                for h in range(parts):
                    to = half // 16 - 1 - tile if REVERSE_SEQ else tile
                    start = pl.multiple_of(to * 256 + h * 16 + place, 16)
                    w_ref[pl.ds(start, 16), :] = source[at : at + 16, h * cols : (h + 1) * cols]
    out_ref[...] = jnp.dot(rows_ref[...], w_ref[...], preferred_element_type=F32).astype(BF16)


def lay_out_kernel(back_ref, out_hbm, sems):
    blocks, _, cols = back_ref.shape
    stores = [
        pltpu.make_async_copy(back_ref.at[i], out_hbm.at[:, pl.ds(i * cols, cols)], sems.at[i])
        for i in range(blocks)
    ]
    for copy in stores:
        copy.start()
    for copy in stores:
        copy.wait()


def step(grad_out, pre_act, word_of, word_owner, w_proj):
    n_seq = lax.axis_size("seq")
    n_doc = lax.axis_size("doc")
    n_chip = n_seq // 2
    bytes_here, width = grad_out.shape[1:]
    per_owner = word_owner.shape[1] // n_seq
    depth, cols = w_proj.shape
    part = width + LANES
    total = 2 * width + LANES + depth // 4 * cols
    groups = [
        [32 * y2 + 16 * y1 + 8 * y0 + 2 * x + c for y0 in range(2) for x in range(4)]
        for y2 in range(2)
        for y1 in range(2)
        for c in range(2)
    ]
    chips = list(range(n_chip))[:: -1 if REVERSE_SEQ else 1]
    same_core = [[2 * chip + c for chip in chips] for c in range(2)]
    across = [(i, i ^ 1) for i in range(n_seq)]
    params = pltpu.CompilerParams(vmem_limit_bytes=VMEM_LIMIT)

    hbm = pl.BlockSpec(memory_space=pltpu.HBM)
    vmem = pl.BlockSpec(memory_space=pltpu.VMEM)
    *inputs, w_sent = pl.pallas_call(
        load_kernel,
        out_shape=[
            jax.ShapeDtypeStruct(word_of.shape, word_of.dtype),
            jax.ShapeDtypeStruct((1, LANES), word_owner.dtype),
            jax.ShapeDtypeStruct((bytes_here, width), BF16),
            jax.ShapeDtypeStruct((bytes_here, width), BF16),
            jax.ShapeDtypeStruct((n_doc, depth // 2, cols), BF16),
        ],
        in_specs=[hbm] * 5,
        out_specs=[vmem] * 4 + [hbm],
        scratch_shapes=[
            pltpu.VMEM((depth, cols), BF16),
            pltpu.SemaphoreType.DMA((5 + n_doc,)),
        ],
        compiler_params=params,
        cost_estimate=pl.CostEstimate(flops=0, bytes_accessed=2_000_000, transcendentals=0),
        name="load",
    )(
        *(
            pltpu.with_memory_space_constraint(x, pltpu.HBM)
            for x in (word_of, word_owner, grad_out[0], pre_act[0], w_proj)
        )
    )
    w_docs = lax.all_to_all(
        w_sent, "doc", 0, 0, tiled=True,
        axis_index_groups=[list(DOC_ORDER)],
    )
    keep, send = pl.pallas_call(
        lambda *refs: word_sums_kernel(n_seq, *refs),
        out_shape=[jax.ShapeDtypeStruct((n_seq, part), BF16)] * 2,
        in_specs=[vmem] * 4,
        out_specs=[vmem] * 2,
        compiler_params=params,
        cost_estimate=pl.CostEstimate(flops=20_000_000, bytes_accessed=3_000_000, transcendentals=500_000),
        name="word_sums",
    )(*inputs)
    other = lax.ppermute(send, "seq", across)
    packed = pl.pallas_call(
        pack_kernel,
        out_shape=jax.ShapeDtypeStruct((n_seq, total), BF16),
        compiler_params=params,
        cost_estimate=pl.CostEstimate(flops=20_000_000, bytes_accessed=1_000_000, transcendentals=0),
        name="pack",
    )(keep, other, w_docs)
    got = lax.all_to_all(
        packed.reshape(n_chip, 2, total), "seq", 0, 0, tiled=True, axis_index_groups=same_core
    ).reshape(n_seq, total)

    rows = pl.pallas_call(
        lambda *refs: own_rows_kernel(per_owner, width, *refs),
        out_shape=jax.ShapeDtypeStruct((n_doc, per_owner, width), BF16),
        compiler_params=params,
        cost_estimate=pl.CostEstimate(flops=20_000_000, bytes_accessed=1_500_000, transcendentals=0),
        name="own_rows",
    )(got)
    rows = lax.all_to_all(rows, "seq", 0, 0, tiled=True, axis_index_groups=groups)

    mine = got[:, 2 * width + LANES :]
    theirs = lax.ppermute(mine, "doc", [(i, i ^ 1) for i in range(n_doc)])
    mine = jnp.concatenate([mine, theirs], axis=0)
    theirs = lax.ppermute(mine, "seq", across)

    out = pl.pallas_call(
        project_kernel,
        out_shape=jax.ShapeDtypeStruct((n_doc * per_owner, cols), BF16),
        scratch_shapes=[pltpu.VMEM((width, cols), BF16)],
        compiler_params=params,
        cost_estimate=pl.CostEstimate(flops=600_000_000, bytes_accessed=2_500_000, transcendentals=0),
        name="project",
    )(rows.reshape(n_doc * per_owner, width), mine, theirs)
    back = lax.all_to_all(
        out.reshape(n_doc, per_owner, cols), "seq", 0, 0, tiled=True, axis_index_groups=groups
    )
    out = pl.pallas_call(
        lay_out_kernel,
        out_shape=jax.ShapeDtypeStruct((per_owner, n_doc * cols), BF16),
        in_specs=[vmem],
        out_specs=hbm,
        scratch_shapes=[pltpu.SemaphoreType.DMA((n_doc,))],
        compiler_params=params,
        name="lay_out",
    )(back)
    return out[None]


DOC_ORDER = (7, 0, 6, 1, 5, 2, 4, 3)
REVERSE_SEQ = True
VMEM_LIMIT = 16 * 1024 * 1024


def solution(mesh):
    return jax.shard_map(
        step,
        mesh=mesh,
        in_specs=(
            P("doc", "seq", None),
            P("doc", "seq", None),
            P("doc", "seq"),
            P("doc", None),
            P("seq", "doc"),
        ),
        out_specs=P("doc", "seq", None),
        check_vma=False,
    )
```

```python
import jax
import jax.numpy as jnp
from jax import lax
from jax.experimental import pallas as pl
from jax.experimental.pallas import tpu as pltpu
from jax.sharding import PartitionSpec as P


inv_root_two = 0.7071067811865476
inv_root_tau = 0.3989422804014327
BF16 = jnp.bfloat16
F32 = jnp.float32
LANES = 128


def slope_of(value):
    return (
        0.5 * (1.0 + lax.erf(value * inv_root_two))
        + value * jnp.exp(-0.5 * value * value) * inv_root_tau
    )


def listed(index, values):
    return sum(jnp.where(index == i, value, 0) for i, value in enumerate(values))


def chip_at(place):
    return listed(place // 8, OUTER) * 8 + listed(place % 8, INNER)


def load_kernel(word_hbm, owner_hbm, grad_hbm, pre_hbm, w_hbm, word_ref, owner_ref, grad_ref, pre_ref, sent_hbm, w_ref, sems):
    half = w_ref.shape[0] // 2
    first = [pltpu.make_async_copy(w_hbm, w_ref, sems.at[0])]
    loads = [
        pltpu.make_async_copy(word_hbm, word_ref, sems.at[1]),
        pltpu.make_async_copy(owner_hbm.at[:, :LANES], owner_ref, sems.at[2]),
        pltpu.make_async_copy(pre_hbm, pre_ref, sems.at[3]),
        pltpu.make_async_copy(grad_hbm, grad_ref, sems.at[4]),
    ]
    for copy in first:
        copy.start()
    for copy in loads:
        copy.start()
    for copy in first:
        copy.wait()
    stores = [
        pltpu.make_async_copy(w_ref.at[pl.ds(d % 2 * half, half), :], sent_hbm.at[i], sems.at[5 + i])
        for i, d in enumerate(DOC_ORDER)
    ]
    for copy in stores:
        copy.start()
    for copy in loads + stores:
        copy.wait()


def word_sums_kernel(n_seq, word_ref, owner_ref, grad_ref, pre_ref, keep_ref, send_ref):
    half = n_seq
    width = grad_ref.shape[1]
    step = 2 * LANES
    chunks = width // step
    source = lax.broadcasted_iota(jnp.int32, (step, step), 0)
    target = lax.broadcasted_iota(jnp.int32, (step, step), 1)
    moved = (
        source // 16 % 2 * 128
        + source // 8 % 2 * 64
        + source // 2 % 4 * 16
        + listed(source // 32, [INNER.index(i) for i in range(8)]) * 2
        + source % 2
    )
    order = jnp.where(moved == target, 1.0, 0.0).astype(BF16)
    core = lax.axis_index("seq") % 2
    row = lax.broadcasted_iota(jnp.int32, (2 * half, LANES), 0)
    lane = lax.broadcasted_iota(jnp.int32, (2 * half, LANES), 1)
    owner = chip_at(row % half // 2) * 2 + (core ^ row // half)
    words = word_ref[...]
    rank = words // n_seq
    owned = (owner_ref[...] == owner) & (lane < n_seq)
    remainder = jnp.sum(jnp.where(owned, lane, 0).astype(F32), axis=1, keepdims=True)
    parity = lax.broadcasted_iota(jnp.int32, (2 * half, 1), 0) % 2
    match = (words % n_seq == remainder.astype(jnp.int32)) & (rank % 2 == parity)
    ids = jnp.max(jnp.where(match, rank, 0).astype(F32), axis=1, keepdims=True)
    picks = jnp.where(match, 1.0, 0.0).astype(BF16)
    wide = jnp.broadcast_to(ids, (2 * half, LANES)).astype(BF16)
    keep_ref[:, width:] = wide[:half]
    send_ref[:, width:] = wide[half:]
    for chunk in range(chunks):
        cols = slice(chunk * step, (chunk + 1) * step)
        g_pre = (grad_ref[:, cols].astype(F32) * slope_of(pre_ref[:, cols].astype(F32))).astype(BF16)
        summed = jnp.dot(picks, g_pre, preferred_element_type=F32).astype(BF16)
        summed = jnp.dot(summed, order, preferred_element_type=F32).astype(BF16)
        keep_ref[:, cols] = summed[:half]
        send_ref[:, cols] = summed[half:]


def pack_kernel(keep_ref, other_ref, w_ref, out_ref):
    rows = keep_ref.shape[0]
    width = keep_ref.shape[1] - LANES
    blocks, depth, cols = w_ref.shape
    out_ref[:, :width] = keep_ref[:, :width]
    out_ref[:, width : 2 * width] = other_ref[:, :width]
    lane = lax.broadcasted_iota(jnp.int32, (rows, LANES), 1)
    ids = [ref[:, width:].astype(F32) for ref in (keep_ref, other_ref)]
    out_ref[:, 2 * width : 2 * width + LANES] = jnp.where(lane < rows, *ids).astype(BF16)
    out_row = lax.broadcasted_iota(jnp.int32, (rows, blocks * depth), 0)
    w_row = lax.broadcasted_iota(jnp.int32, (rows, blocks * depth), 1)
    chip = chip_at(out_row // 2)
    block = chip // 4 % 2 * 4 + chip % 4
    place = listed(block, [DOC_ORDER.index(d) for d in range(blocks)])
    first = place * depth + out_row % 2
    flat = w_ref[...].astype(F32).reshape(blocks * depth, cols).astype(BF16)
    for h in range(depth // 2):
        chosen = jnp.where(w_row == first + 2 * h, 1.0, 0.0).astype(BF16)
        at = 2 * width + LANES + h * cols
        out_ref[:, at : at + cols] = jnp.dot(
            chosen, flat, preferred_element_type=F32
        ).astype(BF16)


def own_rows_kernel(per_owner, width, got_ref, out_ref):
    slots = got_ref.shape[0]
    slot = lax.broadcasted_iota(jnp.int32, (slots, LANES), 0)
    lane = lax.broadcasted_iota(jnp.int32, (slots, LANES), 1)
    wide = got_ref[:, 2 * width : 2 * width + LANES].astype(F32)
    ids = jnp.sum(jnp.where(slot == lane % slots, wide, 0.0), axis=0, keepdims=True)
    rows = lax.broadcasted_iota(jnp.int32, (per_owner, LANES), 0)
    picks = jnp.where(rows == ids.astype(jnp.int32), 1.0, 0.0).astype(BF16)
    summed = jnp.dot(
        picks[:, :slots], got_ref[:, :width], preferred_element_type=F32
    ) + jnp.dot(picks[:, slots:], got_ref[:, width : 2 * width], preferred_element_type=F32)
    summed = summed.astype(BF16)
    for copy in range(out_ref.shape[0]):
        out_ref[copy] = summed


def project_kernel(rows_ref, mine_ref, theirs_ref, out_ref, w_ref):
    cols = w_ref.shape[1]
    parts = mine_ref.shape[1] // cols
    half = mine_ref.shape[0] // 2
    core = lax.axis_index("seq") % 2
    plane = lax.axis_index("doc") % 2
    for c, source in enumerate((mine_ref, theirs_ref)):
        for z in range(2):
            place = (core ^ c) * 128 + (plane ^ z) * 64
            for tile in range(half // 16):
                at = z * half + tile * 16
                for h in range(parts):
                    to = OUTER[tile]
                    start = pl.multiple_of(to * 256 + h * 16 + place, 16)
                    w_ref[pl.ds(start, 16), :] = source[at : at + 16, h * cols : (h + 1) * cols]
    out_ref[...] = jnp.dot(rows_ref[...], w_ref[...], preferred_element_type=F32).astype(BF16)


def lay_out_kernel(back_ref, out_hbm, sems):
    blocks, _, cols = back_ref.shape
    stores = [
        pltpu.make_async_copy(back_ref.at[i], out_hbm.at[:, pl.ds(i * cols, cols)], sems.at[i])
        for i in range(blocks)
    ]
    for copy in stores:
        copy.start()
    for copy in stores:
        copy.wait()


def step(grad_out, pre_act, word_of, word_owner, w_proj):
    n_seq = lax.axis_size("seq")
    n_doc = lax.axis_size("doc")
    n_chip = n_seq // 2
    bytes_here, width = grad_out.shape[1:]
    per_owner = word_owner.shape[1] // n_seq
    depth, cols = w_proj.shape
    part = width + LANES
    total = 2 * width + LANES + depth // 4 * cols
    groups = [
        [32 * y2 + 16 * y1 + 8 * y0 + 2 * x + c for y0 in range(2) for x in range(4)]
        for y2 in range(2)
        for y1 in range(2)
        for c in range(2)
    ]
    chips = [8 * outer + inner for outer in OUTER for inner in INNER]
    same_core = [[2 * chip + c for chip in chips] for c in range(2)]
    across = [(i, i ^ 1) for i in range(n_seq)]
    params = pltpu.CompilerParams(vmem_limit_bytes=VMEM_LIMIT)

    hbm = pl.BlockSpec(memory_space=pltpu.HBM)
    vmem = pl.BlockSpec(memory_space=pltpu.VMEM)
    *inputs, w_sent = pl.pallas_call(
        load_kernel,
        out_shape=[
            jax.ShapeDtypeStruct(word_of.shape, word_of.dtype),
            jax.ShapeDtypeStruct((1, LANES), word_owner.dtype),
            jax.ShapeDtypeStruct((bytes_here, width), BF16),
            jax.ShapeDtypeStruct((bytes_here, width), BF16),
            jax.ShapeDtypeStruct((n_doc, depth // 2, cols), BF16),
        ],
        in_specs=[hbm] * 5,
        out_specs=[vmem] * 4 + [hbm],
        scratch_shapes=[
            pltpu.VMEM((depth, cols), BF16),
            pltpu.SemaphoreType.DMA((5 + n_doc,)),
        ],
        compiler_params=params,
        cost_estimate=pl.CostEstimate(flops=0, bytes_accessed=2_000_000, transcendentals=0),
        name="load",
    )(
        *(
            pltpu.with_memory_space_constraint(x, pltpu.HBM)
            for x in (word_of, word_owner, grad_out[0], pre_act[0], w_proj)
        )
    )
    w_docs = lax.all_to_all(
        w_sent, "doc", 0, 0, tiled=True,
        axis_index_groups=[list(DOC_ORDER)],
    )
    keep, send = pl.pallas_call(
        lambda *refs: word_sums_kernel(n_seq, *refs),
        out_shape=[jax.ShapeDtypeStruct((n_seq, part), BF16)] * 2,
        in_specs=[vmem] * 4,
        out_specs=[vmem] * 2,
        compiler_params=params,
        cost_estimate=pl.CostEstimate(flops=20_000_000, bytes_accessed=3_000_000, transcendentals=500_000),
        name="word_sums",
    )(*inputs)
    other = lax.ppermute(send, "seq", across)
    packed = pl.pallas_call(
        pack_kernel,
        out_shape=jax.ShapeDtypeStruct((n_seq, total), BF16),
        compiler_params=params,
        cost_estimate=pl.CostEstimate(flops=20_000_000, bytes_accessed=1_000_000, transcendentals=0),
        name="pack",
    )(keep, other, w_docs)
    got = lax.all_to_all(
        packed.reshape(n_chip, 2, total), "seq", 0, 0, tiled=True, axis_index_groups=same_core
    ).reshape(n_seq, total)

    rows = pl.pallas_call(
        lambda *refs: own_rows_kernel(per_owner, width, *refs),
        out_shape=jax.ShapeDtypeStruct((n_doc, per_owner, width), BF16),
        compiler_params=params,
        cost_estimate=pl.CostEstimate(flops=20_000_000, bytes_accessed=1_500_000, transcendentals=0),
        name="own_rows",
    )(got)
    rows = lax.all_to_all(rows, "seq", 0, 0, tiled=True, axis_index_groups=groups)

    mine = got[:, 2 * width + LANES :]
    theirs = lax.ppermute(mine, "doc", [(i, i ^ 1) for i in range(n_doc)])
    mine = jnp.concatenate([mine, theirs], axis=0)
    theirs = lax.ppermute(mine, "seq", across)

    out = pl.pallas_call(
        project_kernel,
        out_shape=jax.ShapeDtypeStruct((n_doc * per_owner, cols), BF16),
        scratch_shapes=[pltpu.VMEM((width, cols), BF16)],
        compiler_params=params,
        cost_estimate=pl.CostEstimate(flops=600_000_000, bytes_accessed=2_500_000, transcendentals=0),
        name="project",
    )(rows.reshape(n_doc * per_owner, width), mine, theirs)
    back = lax.all_to_all(
        out.reshape(n_doc, per_owner, cols), "seq", 0, 0, tiled=True, axis_index_groups=groups
    )
    out = pl.pallas_call(
        lay_out_kernel,
        out_shape=jax.ShapeDtypeStruct((per_owner, n_doc * cols), BF16),
        in_specs=[vmem],
        out_specs=hbm,
        scratch_shapes=[pltpu.SemaphoreType.DMA((n_doc,))],
        compiler_params=params,
        name="lay_out",
    )(back)
    return out[None]


DOC_ORDER = (7, 0, 6, 1, 5, 2, 4, 3)
OUTER = (2, 3, 1, 0)
INNER = (7, 6, 5, 4, 3, 2, 1, 0)
VMEM_LIMIT = 16 * 1024 * 1024


def solution(mesh):
    return jax.shard_map(
        step,
        mesh=mesh,
        in_specs=(
            P("doc", "seq", None),
            P("doc", "seq", None),
            P("doc", "seq"),
            P("doc", None),
            P("seq", "doc"),
        ),
        out_specs=P("doc", "seq", None),
        check_vma=False,
    )
```
